1024 devices in a mesh: bag: 64 (over y_lo, z, core), ulysses: 16 (over x, y_hi).
Axes of the slice: x: 8, y: 8 (y_hi: 2, y_lo: 4; y = y_hi * 4 + y_lo), z: 8, core: 2. Of those that a mesh axis runs over, the one named last changes fastest.
Arguments:
- queries: bfloat16 [65536, 4096], P(('bag', 'ulysses')), may hold values from -13 to 13
- keys: bfloat16 [65536, 4096], P(('bag', 'ulysses')), may hold values from -13 to 13
- values: bfloat16 [65536, 4096], P(('bag', 'ulysses')), may hold values from -6 to 6
- span_route: int32 [64, 16, 64], P('bag'), may hold values from 0 to 63, each once within a row
- seq_lengths: int32 [64, 4], P('bag'), may hold values from 1 to 512, 1024 in all within a row
Outputs:
- attended: bfloat16 [65536, 4096], P(('bag', 'ulysses'))
The draws below stay inside these ranges and needn't reach their ends.
Inputs may be any that keep to these rules, and one draw needn't show every extreme that they name: For each b and u, span_route[b, u, 0 to 63] is a permutation of the bags. `seq_lengths`: row B lists bag B's 4 sequence lengths in packed order; each row sums to 1024 and its largest entry is 512.
All inputs are finite; a program needn't handle non-finite values.
Results may differ from the reference program's by a relative error of at most 0.0049.
Values may be sent and summed in bfloat16 or wider, within the bound.
A program may use at most 32 MiB of HBM per device.

```python
import math
import jax
import jax.numpy as jnp
import numpy as np
from jax import lax

HEADS = 32
HDIM = 128
TOK_DEV = 64
SEQ_BAG = 4
TOKENS = 65536
BAG_TOK = 1024
MAX_LEN = 512
N_BAG = 64
N_ULYSSES = 16


def draw_queries(key, part):
    return jnp.clip(jax.random.normal(jax.random.fold_in(key, 11), (TOKENS, HEADS * HDIM), jnp.float32), -6.0, 6.0).astype(jnp.bfloat16)


def draw_keys(key, part):
    return jnp.clip(jax.random.normal(jax.random.fold_in(key, 12), (TOKENS, HEADS * HDIM), jnp.float32), -6.0, 6.0).astype(jnp.bfloat16)


def levels(rng, dims, pieces, smallest, top_value):
    gain, own = 1.0, jax.random.fold_in(rng, 6)
    for dim, blocks in pieces:
        heights = jnp.exp(jax.random.uniform(jax.random.fold_in(own, dim), (blocks,), jnp.float32, smallest / len(pieces), top_value / len(pieces)))
        gain = gain * jnp.repeat(heights, dims[dim] // blocks).reshape([-1 if axis == dim else 1 for axis in range(len(dims))])
    return gain


def length_profile(count, total, most, skew):
    loads = [(1 << 20) // math.isqrt(standing ** skew) + 1 for standing in range(2, count + 1)]
    spare, counts = total - most - (count - 1), [1] * (count - 1)
    while spare > 0:
        movable = [i for i in range(count - 1) if counts[i] < most]
        pool, left = sum([loads[i] for i in movable]), spare
        for i in movable:
            more = min(most - counts[i], max(1, left * loads[i] // pool), spare)
            counts[i] = counts[i] + more
            spare = spare - more
    return np.array([most] + counts)


def uneven_parts(rng, amount, total, reach, skew):
    if amount == 2:
        one = jax.random.randint(rng, (), max(1, total - reach), min(reach, total - 1) + 1)
        return jnp.stack([one, total - one])
    tallies = jnp.asarray(length_profile(amount, total, reach, skew), jnp.int32)
    pairs = (amount - 1) // 2
    giver, receiver = tallies[1:1 + 2 * pairs:2], tallies[2:2 + 2 * pairs:2]
    margin = jnp.minimum(giver - 1, reach - receiver)
    moved = jax.random.randint(jax.random.fold_in(rng, 1), (pairs,), 0, 1 << 20) % (margin + 1)
    tallies = tallies.at[1:1 + 2 * pairs:2].set(giver - moved).at[2:2 + 2 * pairs:2].set(receiver + moved)
    return tallies[jax.random.permutation(jax.random.fold_in(rng, 2), amount)]


def noise(own_key, extent, width, reach, cuts=(), kind=jnp.bfloat16):
    entries = width * jax.random.normal(own_key, extent, jnp.float32)
    if cuts:
        entries = entries * levels(own_key, extent, cuts, -0.22, 0.18)
    return jnp.clip(entries, -reach, reach).astype(kind)


def setup_inputs(seed: int = 0) -> dict:
    key_of = jax.random.split(jax.random.key(seed), 6)
    return {
        "queries": draw_queries(jax.random.fold_in(key_of[5], 71), 0),
        "keys": draw_keys(jax.random.fold_in(key_of[5], 71), 0),
        "values": noise(key_of[2], (TOKENS, HEADS * HDIM), 1.0, 6.0, ((0, 1024),)),
        "span_route": jax.vmap(lambda own: jax.random.permutation(own, N_BAG))(jax.random.split(key_of[3], N_BAG * N_ULYSSES)).reshape((N_BAG, N_ULYSSES, N_BAG)).astype(jnp.int32),
        "seq_lengths": jax.vmap(lambda own: uneven_parts(own, SEQ_BAG, BAG_TOK, MAX_LEN, 2))(jax.random.split(key_of[4], N_BAG)).reshape((N_BAG, SEQ_BAG)).astype(jnp.int32),
    }


def attend_bag(operands):
    query_bag, key_bag, value_bag, lengths = operands
    bag_tok = query_bag.shape[0]
    seq_ends = jnp.cumsum(lengths).astype(jnp.int32)
    positions = jnp.arange(bag_tok, dtype=jnp.int32)
    sequence = lax.optimization_barrier(jnp.sum((positions[:, None] >= seq_ends[None, :]).astype(jnp.int32), axis=1))
    same_seq = sequence[:, None] == sequence[None, :]
    query_f = query_bag.reshape(bag_tok, HEADS, HDIM).astype(jnp.float32)
    key_f = key_bag.reshape(bag_tok, HEADS, HDIM).astype(jnp.float32)
    value_f = value_bag.reshape(bag_tok, HEADS, HDIM).astype(jnp.float32)
    scores = jnp.einsum('qhd,khd->hqk', query_f, key_f) * (1.0 / math.sqrt(HDIM))
    scores = jnp.where(same_seq[None, :, :], scores, -jnp.inf)
    row_max = lax.optimization_barrier(jnp.max(scores, axis=-1, keepdims=True))
    expo = jnp.exp(scores - row_max)
    weights = (expo / lax.optimization_barrier(jnp.sum(expo, axis=-1, keepdims=True))).astype(jnp.bfloat16)
    output = jnp.einsum('hqk,khd->qhd', weights.astype(jnp.float32), value_f)
    return output.astype(jnp.bfloat16).reshape(bag_tok, HEADS * HDIM)

def reference(queries, keys, values, span_route, seq_lengths):
    span_len = TOK_DEV // N_BAG
    bag_tok = TOK_DEV * N_ULYSSES
    row_width = HEADS * HDIM
    inverse = jnp.argsort(span_route, axis=-1).astype(jnp.int32)
    dest_idx = jnp.arange(N_BAG, dtype=jnp.int32)[:, None, None, None]
    group_idx = jnp.arange(N_ULYSSES, dtype=jnp.int32)[None, :, None, None]
    source_idx = jnp.arange(N_BAG, dtype=jnp.int32)[None, None, :, None]
    offset_idx = jnp.arange(span_len, dtype=jnp.int32)[None, None, None, :]
    span_idx = inverse[source_idx, group_idx, dest_idx]
    token_idx = ((source_idx * N_ULYSSES + group_idx) * TOK_DEV + span_idx * span_len + offset_idx).astype(jnp.int32)
    token_idx = token_idx.reshape(N_BAG, bag_tok)
    packed_q = queries[token_idx]
    packed_k = keys[token_idx]
    packed_v = values[token_idx]
    packed_out = lax.map(attend_bag, (packed_q, packed_k, packed_v, seq_lengths))
    owner_bag = jnp.arange(N_BAG, dtype=jnp.int32)[:, None, None, None]
    owner_group = jnp.arange(N_ULYSSES, dtype=jnp.int32)[None, :, None, None]
    destination = span_route[:, :, :, None]
    flat_idx = (destination * bag_tok + (owner_group * N_BAG + owner_bag) * span_len + offset_idx).astype(jnp.int32)
    flat_idx = flat_idx.reshape(TOKENS)
    return packed_out.reshape(N_BAG * bag_tok, row_width)[flat_idx]
```

```python
import functools
import math

import jax
import jax.numpy as jnp
from jax import lax
from jax.experimental import pallas as pl
from jax.experimental.pallas import tpu as pltpu
from jax.sharding import PartitionSpec as P

HEADS = 32
HDIM = 128
NX, NY, NZ = 8, 8, 16
UNIT = (2, HDIM)
BLOCK = (NX, NY, NZ) + UNIT
MESH = pl.DeviceIdType.MESH
VMEM = pl.BlockSpec(memory_space=pltpu.VMEM)
SMEM = pl.BlockSpec(memory_space=pltpu.SMEM)


def pack_kernel(route_ref, *refs):
    ins, outs = refs[:3], refs[3:]
    lane_route = jnp.concatenate([route_ref[...], route_ref[...]], axis=1)
    row = lax.broadcasted_iota(jnp.int32, (128, 128), 0)
    lane = lax.broadcasted_iota(jnp.int32, (128, 128), 1)
    pick = ((lane_route == row // 2) & (lane // 64 == row % 2)).astype(jnp.bfloat16)
    for i_ref, o_ref in zip(ins, outs):
        for u in range(16):
            pair = jnp.concatenate(
                [i_ref[:, u * 256 : u * 256 + 128], i_ref[:, u * 256 + 128 : u * 256 + 256]], axis=0
            )
            rows = jnp.dot(pick, pair, preferred_element_type=jnp.float32)
            o_ref[u * 128 : (u + 1) * 128, :] = rows.astype(jnp.bfloat16)


def unpack_kernel(route_ref, i_ref, o_ref):
    col = route_ref[...]
    lane = lax.broadcasted_iota(jnp.int32, (64, 128), 1)
    picks = [(lane == col * 2 + h).astype(jnp.bfloat16) for h in (0, 1)]
    pick = jnp.concatenate(picks, axis=0)
    for u in range(16):
        both = jnp.dot(
            pick, i_ref[u * 128 : (u + 1) * 128, :], preferred_element_type=jnp.float32
        ).astype(jnp.bfloat16)
        o_ref[:, u * 256 : u * 256 + 128] = both[:64]
        o_ref[:, u * 256 + 128 : u * 256 + 256] = both[64:]


def place():
    b = lax.axis_index("bag")
    u = lax.axis_index("ulysses")
    return {"x": u // 2, "y": (u % 2) * 4 + b // 16, "z": b % 16}


def device(here, axis, t):
    at = dict(here)
    at[axis] = t
    return ((at["y"] % 4) * 16 + at["z"], at["x"] * 2 + at["y"] // 4)


def slot(ref, axis, t):
    if axis == "x":
        return ref.at[t]
    if axis == "y":
        return ref.at[:, t]
    return ref.at[:, :, t]


SIZE = {"x": NX, "y": NY, "z": NZ}
STEPS = {"x": (4, 3, 5, 2, 6, 1, 7), "y": (4, 3, 5, 2, 6, 1, 7)}
STEPS["z"] = (8, 9, 7, 6, 10, 5, 11, 4, 12, 3, 13, 2, 14, 1, 15)


def exchange_start(axis, here, src, dst, send, recv, own):
    mine = here[axis]
    for step in STEPS[axis]:
        t = (mine + step) % SIZE[axis]
        pltpu.make_async_remote_copy(
            src_ref=slot(src, axis, t),
            dst_ref=slot(dst, axis, mine),
            send_sem=send,
            recv_sem=recv,
            device_id=device(here, axis, t),
            device_id_type=MESH,
        ).start()
    pltpu.make_async_copy(slot(src, axis, mine), slot(dst, axis, mine), own).start()


def exchange_wait(axis, here, src, dst, send, recv, own):
    mine = here[axis]
    part = slot(dst, axis, pl.ds(0, SIZE[axis] - 1))
    pltpu.make_async_copy(part, part, recv).wait()
    pltpu.make_async_copy(part, part, send).wait()
    pltpu.make_async_copy(slot(src, axis, mine), slot(dst, axis, mine), own).wait()


def exchange_kernel(orders, *refs):
    n = len(orders)
    bufs = [refs[:n], refs[2 * n : 3 * n], refs[3 * n : 4 * n], refs[n : 2 * n]]
    send, recv, own = refs[4 * n :]
    here = place()
    barrier = pltpu.get_barrier_semaphore()
    for axis in "xyz":
        for step in STEPS[axis]:
            t = (here[axis] + step) % SIZE[axis]
            pl.semaphore_signal(
                barrier, inc=1, device_id=device(here, axis, t), device_id_type=MESH
            )
    pl.semaphore_wait(barrier, sum(len(steps) for steps in STEPS.values()))
    for stage in range(3):
        for i in range(n):
            exchange_start(
                orders[i][stage], here, bufs[stage][i], bufs[stage + 1][i],
                send.at[i, stage], recv.at[i, stage], own.at[i, stage],
            )
        for i in range(n):
            exchange_wait(
                orders[i][stage], here, bufs[stage][i], bufs[stage + 1][i],
                send.at[i, stage], recv.at[i, stage], own.at[i, stage],
            )


def exchange(orders, collective_id, *arrays):
    n = len(orders)
    shape = jax.ShapeDtypeStruct(BLOCK, jnp.bfloat16)
    return pl.pallas_call(
        functools.partial(exchange_kernel, orders),
        out_shape=[shape] * n,
        in_specs=[VMEM] * n,
        out_specs=[VMEM] * n,
        scratch_shapes=[pltpu.VMEM(BLOCK, jnp.bfloat16)] * (2 * n)
        + [pltpu.SemaphoreType.DMA((n, 3))] * 3,
        compiler_params=pltpu.CompilerParams(has_side_effects=True, collective_id=collective_id),
        name="exchange_" + "_".join(orders),
    )(*[a.reshape(BLOCK) for a in arrays])


def attend_kernel(len_ref, q_ref, k_ref, v_ref, o_ref, qf, kf, vf, of):
    tok = q_ref.shape[0] // 2
    rows = 256
    scale = 1.0 / math.sqrt(HDIM)
    qf[...] = q_ref[...].astype(jnp.float32)
    kf[...] = k_ref[...].astype(jnp.float32)
    vf[...] = v_ref[...].astype(jnp.float32)
    ends = [len_ref[0, 0]]
    for e in range(1, 4):
        ends.append(ends[-1] + len_ref[0, e])

    def sequence(shape, axis, first):
        p = lax.broadcasted_iota(jnp.int32, shape, axis) + first
        return sum((p >= e).astype(jnp.int32) for e in ends)

    key_seq = sequence((1, tok), 1, 0)
    for h in range(2):
        keys = kf[pl.ds(h, tok, stride=2), :].astype(jnp.bfloat16)
        values = vf[pl.ds(h, tok, stride=2), :].astype(jnp.bfloat16)

        def one(i, _, h=h, keys=keys, values=values):
            first = pl.multiple_of(i * rows, rows)
            q = qf[pl.ds(first * 2 + h, rows, stride=2), :].astype(jnp.bfloat16)
            s = lax.dot_general(
                q, keys, (((1,), (1,)), ((), ())), preferred_element_type=jnp.float32
            ) * scale
            same = sequence((rows, 1), 0, first) == key_seq
            s = jnp.where(same, s, -jnp.inf)
            e = jnp.exp(s - jnp.max(s, axis=1, keepdims=True))
            w = (e / jnp.sum(e, axis=1, keepdims=True)).astype(jnp.bfloat16)
            o = jnp.dot(w, values, preferred_element_type=jnp.float32)
            of[pl.ds(first * 2 + h, rows, stride=2), :] = o
            return 0

        lax.fori_loop(0, tok // rows, one, 0)
    o_ref[...] = of[...].astype(jnp.bfloat16)


def shards(queries, keys, values, span_route, seq_lengths):
    route = lax.dynamic_index_in_dim(span_route[0], lax.axis_index("ulysses"), 0, keepdims=True)
    rows = jax.ShapeDtypeStruct((2048, HDIM), jnp.bfloat16)
    units = pl.pallas_call(
        pack_kernel, out_shape=[rows] * 3, in_specs=[VMEM] * 4, out_specs=[VMEM] * 3, name="pack"
    )(route, queries, keys, values)
    q, k, v = exchange(("xyz", "yzx", "zxy"), 1, *units)
    wide = pltpu.VMEM((2048, HDIM), jnp.float32)
    attended = pl.pallas_call(
        attend_kernel,
        out_shape=rows,
        in_specs=[SMEM] + [VMEM] * 3,
        out_specs=VMEM,
        scratch_shapes=[wide] * 4,
        name="attend",
    )(seq_lengths, *[a.reshape(2048, HDIM) for a in (q, k, v)])
    (back,) = exchange(("xyz",), 2, attended)
    return pl.pallas_call(
        unpack_kernel,
        out_shape=jax.ShapeDtypeStruct(queries.shape, jnp.bfloat16),
        in_specs=[VMEM] * 2,
        out_specs=VMEM,
        name="unpack",
    )(route.reshape(64, 1), back.reshape(2048, HDIM))


def solution(mesh):
    placed = (
        P(("bag", "ulysses"), None),
        P(("bag", "ulysses"), None),
        P(("bag", "ulysses"), None),
        P("bag", None, None),
        P("bag", None),
    )
    return jax.shard_map(
        shards, mesh=mesh, in_specs=placed, out_specs=P(("bag", "ulysses"), None), check_vma=False
    )
```

```python
import math

import jax
import jax.numpy as jnp
from jax import lax
from jax.experimental import pallas as pl
from jax.experimental.pallas import tpu as pltpu
from jax.sharding import PartitionSpec as P

HEADS = 32
HDIM = 128
NX, NY, NZ = 8, 8, 16
TOK = NX * NY * NZ
BIG = 1e30
UNIT = (2, HDIM)
BLOCK = (NX, NY, NZ) + UNIT
MESH = pl.DeviceIdType.MESH
VMEM = pl.BlockSpec(memory_space=pltpu.VMEM)
SMEM = pl.BlockSpec(memory_space=pltpu.SMEM)


def pick_rows(route):
    lane_route = jnp.concatenate([route, route], axis=1)
    row = lax.broadcasted_iota(jnp.int32, (128, 128), 0)
    lane = lax.broadcasted_iota(jnp.int32, (128, 128), 1)
    return ((lane_route == row // 2) & (lane // 64 == row % 2)).astype(jnp.float32)


def place():
    b = lax.axis_index("bag")
    u = lax.axis_index("ulysses")
    return {"x": u // 2, "y": (u % 2) * 4 + b // 16, "z": b % 16}


def device(here, axis, t):
    at = dict(here)
    at[axis] = t
    return ((at["y"] % 4) * 16 + at["z"], at["x"] * 2 + at["y"] // 4)


def slot(ref, axis, t):
    if axis == "x":
        return ref.at[t]
    if axis == "y":
        return ref.at[:, t]
    return ref.at[:, :, t]


SIZE = {"x": NX, "y": NY, "z": NZ}
STEPS = {"x": (4, 3, 5, 2, 6, 1, 7), "y": (4, 3, 5, 2, 6, 1, 7)}
STEPS["z"] = (8, 9, 7, 6, 10, 5, 11, 4, 12, 3, 13, 2, 14, 1, 15)
ORDERS = ("xyz", "yzx", "zxy")


def send_slots(axis, here, src, dst, send, recv, own):
    mine = here[axis]
    for step in STEPS[axis]:
        t = (mine + step) % SIZE[axis]
        pltpu.make_async_remote_copy(
            src_ref=slot(src, axis, t),
            dst_ref=slot(dst, axis, mine),
            send_sem=send,
            recv_sem=recv,
            device_id=device(here, axis, t),
            device_id_type=MESH,
        ).start()
    pltpu.make_async_copy(slot(src, axis, mine), slot(dst, axis, mine), own).start()


def wait_slots(axis, here, src, dst, send, recv, own):
    mine = here[axis]
    part = slot(dst, axis, pl.ds(0, SIZE[axis] - 1))
    pltpu.make_async_copy(part, part, recv).wait()
    pltpu.make_async_copy(part, part, send).wait()
    pltpu.make_async_copy(slot(src, axis, mine), slot(dst, axis, mine), own).wait()


def main_kernel(
    len_ref, route_ref, q_ref, k_ref, v_ref, back,
    units, mid1, mid2, fin, wide, out_rows, q_seq, k_seq, o_units, ret1, ret2,
    send, recv, own, rsend, xrecv, yrecv, yown, zrecv, zown,
):
    here = place()
    barrier = pltpu.get_barrier_semaphore()
    for axis in "xyz":
        for step in STEPS[axis]:
            t = (here[axis] + step) % SIZE[axis]
            pl.semaphore_signal(
                barrier, inc=1, device_id=device(here, axis, t), device_id_type=MESH
            )

    pick = pick_rows(route_ref[pl.ds(lax.axis_index("ulysses"), 1), :]).astype(jnp.bfloat16)
    bufs = (units, mid1, mid2, fin)

    def args(i, stage):
        return (
            ORDERS[i][stage], here, bufs[stage].at[i], bufs[stage + 1].at[i],
            send.at[i, stage], recv.at[i, stage], own.at[i, stage],
        )

    for i, in_ref in enumerate((q_ref, k_ref, v_ref)):
        flat = units.at[i].reshape(2 * TOK, HDIM)
        for u in range(16):
            pair = jnp.concatenate(
                [in_ref[:, u * 256 : u * 256 + 128], in_ref[:, u * 256 + 128 : u * 256 + 256]],
                axis=0,
            )
            rows = jnp.dot(pick, pair, preferred_element_type=jnp.float32)
            flat[u * 128 : (u + 1) * 128, :] = rows.astype(jnp.bfloat16)
        if i == 0:
            pl.semaphore_wait(barrier, sum(len(steps) for steps in STEPS.values()))
        send_slots(*args(i, 0))

    pos = lax.broadcasted_iota(jnp.int32, (TOK, HDIM), 0)
    lane = lax.broadcasted_iota(jnp.int32, (TOK, HDIM), 1)
    first = 0
    inside = jnp.zeros((TOK, HDIM), jnp.bool_)
    for e in range(4):
        last = first + len_ref[0, e]
        inside = inside | ((lane == e) & (pos >= first) & (pos < last))
        first = last
    q_seq[...] = jnp.where(inside, 1.0, 0.0).astype(jnp.bfloat16)
    k_seq[...] = jnp.where(inside | (lane >= 4), 0.0, -BIG).astype(jnp.bfloat16)

    for stage in (1, 2):
        for i in range(3):
            wait_slots(*args(i, stage - 1))
            send_slots(*args(i, stage))
    for i in (1, 2, 0):
        wait_slots(*args(i, 2))
        wide[i] = fin.at[i].reshape(2 * TOK, HDIM)[...].astype(jnp.float32)

    x = here["x"]
    factor = math.log2(math.e) / math.sqrt(HDIM)
    flat_out = o_units.reshape(2 * TOK, HDIM)
    heads = []
    for h in range(2):
        keys = wide[1, pl.ds(h, TOK, stride=2), :].astype(jnp.bfloat16)
        values = wide[2, pl.ds(h, TOK, stride=2), :].astype(jnp.bfloat16)
        heads.append((jnp.concatenate([keys, k_seq[...]], axis=1), values))

    def pair_of(i):
        return (x // 2 + 1 + i) % 4

    def came_from(i):
        return (x // 2 + 3 - i) % 4

    def attend(i):
        j = pair_of(i)
        for h, (keys, values) in enumerate(heads):
            q = wide[0, pl.ds(j * 512 + h, 256, stride=2), :].astype(jnp.bfloat16)
            q = jnp.concatenate([q, q_seq[pl.ds(pl.multiple_of(j * 256, 256), 256), :]], axis=1)
            s = lax.dot_general(
                q, keys, (((1,), (1,)), ((), ())), preferred_element_type=jnp.float32
            )
            e = jnp.exp2((s - jnp.max(s, axis=1, keepdims=True)) * factor)
            w = (e * (1.0 / jnp.sum(e, axis=1, keepdims=True))).astype(jnp.bfloat16)
            out_rows[pl.ds(h, 256, stride=2), :] = jnp.dot(
                w, values, preferred_element_type=jnp.float32
            )
        flat_out[pl.ds(pl.multiple_of(j * 512, 512), 512), :] = out_rows[...].astype(jnp.bfloat16)

    def send_x(t):
        pltpu.make_async_remote_copy(
            src_ref=o_units.at[t],
            dst_ref=ret1.at[x],
            send_sem=rsend.at[0],
            recv_sem=xrecv.at[x],
            device_id=device(here, "x", t),
            device_id_type=MESH,
        ).start()

    def forward_y(i):
        j = came_from(i)
        for r in range(2):
            piece = ret1.at[j * 2 + r]
            pltpu.make_async_copy(piece, piece, xrecv.at[j * 2 + r]).wait()
        both = pl.ds(j * 2, 2)
        for step in STEPS["y"]:
            t = (here["y"] + step) % NY
            pltpu.make_async_remote_copy(
                src_ref=ret1.at[both, t],
                dst_ref=ret2.at[both, here["y"]],
                send_sem=rsend.at[1],
                recv_sem=yrecv.at[j],
                device_id=device(here, "y", t),
                device_id_type=MESH,
            ).start()
        pltpu.make_async_copy(
            ret1.at[both, here["y"]], ret2.at[both, here["y"]], yown.at[j]
        ).start()

    def forward_z(i):
        j = came_from(i)
        both = pl.ds(j * 2, 2)
        most = ret2.at[both, pl.ds(0, NY - 1)]
        pltpu.make_async_copy(most, most, yrecv.at[j]).wait()
        pltpu.make_async_copy(
            ret1.at[both, here["y"]], ret2.at[both, here["y"]], yown.at[j]
        ).wait()
        for step in STEPS["z"]:
            t = (here["z"] + step) % NZ
            pltpu.make_async_remote_copy(
                src_ref=ret2.at[both, :, t],
                dst_ref=back.at[both, :, here["z"]],
                send_sem=rsend.at[2],
                recv_sem=zrecv,
                device_id=device(here, "z", t),
                device_id_type=MESH,
            ).start()
        pltpu.make_async_copy(
            ret2.at[both, :, here["z"]], back.at[both, :, here["z"]], zown.at[j]
        ).start()

    def block(i, _):
        attend(i)

        @pl.when(i < 3)
        def _():
            send_x(pair_of(i) * 2)
            send_x(pair_of(i) * 2 + 1)

        @pl.when(i == 3)
        def _():
            send_x(x // 2 * 2 + 1 - x % 2)
            pltpu.make_async_copy(o_units.at[x], ret1.at[x], xrecv.at[x]).start()

        @pl.when(i >= 2)
        def _():
            forward_y(i - 2)

        return 0

    lax.fori_loop(0, 4, block, 0)
    lax.fori_loop(2, 4, lambda i, _: (forward_y(i), 0)[1], 0)
    lax.fori_loop(0, 4, lambda i, _: (forward_z(i), 0)[1], 0)

    for i in range(4):
        j = came_from(i)
        mine = here["z"]
        pltpu.make_async_copy(
            ret2.at[pl.ds(j * 2, 2), :, mine], back.at[pl.ds(j * 2, 2), :, mine], zown.at[j]
        ).wait()
    for n, axis in enumerate("xyz"):
        part = slot(back, axis, pl.ds(0, SIZE[axis] - 1))
        if axis == "z":
            pltpu.make_async_copy(part, part, zrecv).wait()
        pltpu.make_async_copy(part, part, rsend.at[n]).wait()


def unpack_kernel(route_ref, i_ref, o_ref):
    pick = pick_rows(route_ref[pl.ds(lax.axis_index("ulysses"), 1), :]).T.astype(jnp.bfloat16)
    for u in range(16):
        both = jnp.dot(
            pick, i_ref[u * 128 : (u + 1) * 128, :], preferred_element_type=jnp.float32
        ).astype(jnp.bfloat16)
        o_ref[:, u * 256 : u * 256 + 128] = both[:64]
        o_ref[:, u * 256 + 128 : u * 256 + 256] = both[64:]


def shards(queries, keys, values, span_route, seq_lengths):
    route = span_route[0]
    block = pltpu.VMEM(BLOCK, jnp.bfloat16)
    three = pltpu.VMEM((3,) + BLOCK, jnp.bfloat16)
    dma = pltpu.SemaphoreType.DMA
    back = pl.pallas_call(
        main_kernel,
        out_shape=jax.ShapeDtypeStruct(BLOCK, jnp.bfloat16),
        in_specs=[SMEM] + [VMEM] * 4,
        out_specs=VMEM,
        scratch_shapes=[three] * 4
        + [
            pltpu.VMEM((3, 2 * TOK, HDIM), jnp.float32),
            pltpu.VMEM((512, HDIM), jnp.float32),
            pltpu.VMEM((TOK, HDIM), jnp.bfloat16),
            pltpu.VMEM((TOK, HDIM), jnp.bfloat16),
            block, block, block,
            dma((3, 3)), dma((3, 3)), dma((3, 3)),
            dma((3,)), dma((NX,)), dma((4,)), dma((4,)), dma, dma((4,)),
        ],
        compiler_params=pltpu.CompilerParams(has_side_effects=True, collective_id=1),
        name="dispatch_attend_return",
    )(seq_lengths, route, queries, keys, values)
    return pl.pallas_call(
        unpack_kernel,
        out_shape=jax.ShapeDtypeStruct(queries.shape, jnp.bfloat16),
        in_specs=[VMEM] * 2,
        out_specs=VMEM,
        name="unpack",
    )(route, back.reshape(2 * TOK, HDIM))


def solution(mesh):
    placed = (
        P(("bag", "ulysses"), None),
        P(("bag", "ulysses"), None),
        P(("bag", "ulysses"), None),
        P("bag", None, None),
        P("bag", None),
    )
    return jax.shard_map(
        shards, mesh=mesh, in_specs=placed, out_specs=P(("bag", "ulysses"), None), check_vma=False
    )
```

```python
import math

import jax
import jax.numpy as jnp
from jax import lax
from jax.experimental import pallas as pl
from jax.experimental.pallas import tpu as pltpu
from jax.sharding import PartitionSpec as P

HEADS = 32
HDIM = 128
NX, NY, NZ = 8, 8, 16
TOK = NX * NY * NZ
BIG = 1e30
UNIT = (2, HDIM)
BLOCK = (NX, NY, NZ) + UNIT
MESH = pl.DeviceIdType.MESH
VMEM = pl.BlockSpec(memory_space=pltpu.VMEM)
SMEM = pl.BlockSpec(memory_space=pltpu.SMEM)


def pick_rows(route):
    lane_route = jnp.concatenate([route, route], axis=1)
    row = lax.broadcasted_iota(jnp.int32, (128, 128), 0)
    lane = lax.broadcasted_iota(jnp.int32, (128, 128), 1)
    return ((lane_route == row // 2) & (lane // 64 == row % 2)).astype(jnp.float32)


def place():
    b = lax.axis_index("bag")
    u = lax.axis_index("ulysses")
    return {"x": u // 2, "y": (u % 2) * 4 + b // 16, "z": b % 16}


def device(here, axis, t):
    at = dict(here)
    at[axis] = t
    return ((at["y"] % 4) * 16 + at["z"], at["x"] * 2 + at["y"] // 4)


def view(ref, **at):
    return ref.at[tuple(at.get(axis, slice(None)) for axis in "xyz")]


SIZE = {"x": NX, "y": NY, "z": NZ}
STEPS = {"x": (4, 3, 5, 2, 6, 1, 7), "y": (4, 3, 5, 2, 6, 1, 7)}
STEPS["z"] = (8, 9, 7, 6, 10, 5, 11, 4, 12, 3, 13, 2, 14, 1, 15)
ORDERS = ("xyz", "yzx", "zxy")
PARTS = ("xyz", "yzx", "zxy", "zxy")
GROUPS = 4
OFFSETS = (2, 1, 3, 0)


def send_to(here, axis, t, src, dst, send, recv):
    pltpu.make_async_remote_copy(
        src_ref=src,
        dst_ref=dst,
        send_sem=send,
        recv_sem=recv,
        device_id=device(here, axis, t),
        device_id_type=MESH,
    ).start()


def wait_for(ref, sem):
    pltpu.make_async_copy(ref, ref, sem).wait()


def main_kernel(
    len_ref, route_ref, q_ref, k_ref, v_ref, back,
    units, mid1, mid2, fin, wide, out_rows, q_seq, k_seq, o_units, ret1, ret2, ret3,
    send, recv1, recv2, recv3, own1, own2, own3, rsend, rrecv, rown,
):
    here = place()
    barrier = pltpu.get_barrier_semaphore()
    for axis in "xyz":
        for step in STEPS[axis]:
            t = (here[axis] + step) % SIZE[axis]
            pl.semaphore_signal(
                barrier, inc=1, device_id=device(here, axis, t), device_id_type=MESH
            )

    pick = pick_rows(route_ref[pl.ds(lax.axis_index("ulysses"), 1), :]).astype(jnp.bfloat16)

    def whole(axis):
        return view(fin.at[0], **{axis: pl.ds(0, SIZE[axis] - 1)})

    def group(i, off):
        axis = ORDERS[i][0]
        width = SIZE[axis] // GROUPS
        j = (here[axis] // width + GROUPS - off) % GROUPS
        return axis, width, j, pl.ds(j * width, width)

    def send1(i):
        axis = ORDERS[i][0]
        mine, width = here[axis], SIZE[axis] // GROUPS
        at_mine = {axis: mine}
        for off in OFFSETS:
            j = (mine // width + off) % GROUPS
            for r in range(0 if off else 1, width):
                t = j * width + (r if off else (mine + r) % width)
                send_to(
                    here, axis, t, view(units.at[i], **{axis: t}), view(mid1.at[i], **at_mine),
                    send.at[i, 0], recv1.at[i, mine // width],
                )
        copy1(i).start()

    def copy1(i):
        at_mine = {ORDERS[i][0]: here[ORDERS[i][0]]}
        return pltpu.make_async_copy(
            view(units.at[i], **at_mine), view(mid1.at[i], **at_mine), own1.at[i]
        )

    def send2(i, off):
        first, width, j, rows = group(i, off)
        axis = ORDERS[i][1]
        if off:
            wait_for(view(mid1.at[i], **{first: rows}), recv1.at[i, j])
        else:
            wait_for(view(mid1.at[i], **{first: pl.ds(0, width - 1)}), recv1.at[i, j])
            copy1(i).wait()
        for step in STEPS[axis]:
            t = (here[axis] + step) % SIZE[axis]
            send_to(
                here, axis, t, view(mid1.at[i], **{first: rows, axis: t}),
                view(mid2.at[i], **{first: rows, axis: here[axis]}), send.at[i, 1], recv2.at[i, j],
            )
        copy2(i, off).start()

    def copy2(i, off):
        first, _, j, rows = group(i, off)
        at = {first: rows, ORDERS[i][1]: here[ORDERS[i][1]]}
        return pltpu.make_async_copy(view(mid1.at[i], **at), view(mid2.at[i], **at), own2.at[i, j])

    def send3(i, off):
        first, _, j, rows = group(i, off)
        second, axis = ORDERS[i][1:]
        wait_for(view(mid2.at[i], **{first: rows, second: pl.ds(0, SIZE[second] - 1)}), recv2.at[i, j])
        copy2(i, off).wait()
        for step in STEPS[axis]:
            t = (here[axis] + step) % SIZE[axis]
            send_to(
                here, axis, t, view(mid2.at[i], **{first: rows, axis: t}),
                view(fin.at[i], **{first: rows, axis: here[axis]}), send.at[i, 2], recv3.at[i],
            )
        copy3(i, off).start()

    def copy3(i, off):
        first, _, j, rows = group(i, off)
        at = {first: rows, ORDERS[i][2]: here[ORDERS[i][2]]}
        return pltpu.make_async_copy(view(mid2.at[i], **at), view(fin.at[i], **at), own3.at[i, j])

    for i, in_ref in enumerate((q_ref, k_ref, v_ref)):
        flat = units.at[i].reshape(2 * TOK, HDIM)
        for u in range(16):
            pair = jnp.concatenate(
                [in_ref[:, u * 256 : u * 256 + 128], in_ref[:, u * 256 + 128 : u * 256 + 256]],
                axis=0,
            )
            rows = jnp.dot(pick, pair, preferred_element_type=jnp.float32)
            flat[u * 128 : (u + 1) * 128, :] = rows.astype(jnp.bfloat16)
        if i == 0:
            pl.semaphore_wait(barrier, sum(len(steps) for steps in STEPS.values()))
        send1(i)

    pos = lax.broadcasted_iota(jnp.int32, (TOK, HDIM), 0)
    lane = lax.broadcasted_iota(jnp.int32, (TOK, HDIM), 1)
    first = 0
    inside = jnp.zeros((TOK, HDIM), jnp.bool_)
    for e in range(4):
        last = first + len_ref[0, e]
        inside = inside | ((lane == e) & (pos >= first) & (pos < last))
        first = last
    q_seq[...] = jnp.where(inside, 1.0, 0.0).astype(jnp.bfloat16)
    k_seq[...] = jnp.where(inside | (lane >= 4), 0.0, -BIG).astype(jnp.bfloat16)

    for send_on in (send2, send3):
        for off in OFFSETS:
            for i in range(3):
                send_on(i, off)
    for i in (1, 2, 0):
        wait_for(whole(ORDERS[i][2]), recv3.at[i])
        for off in OFFSETS:
            copy3(i, off).wait()
        wide[i] = fin.at[i].reshape(2 * TOK, HDIM)[...].astype(jnp.float32)

    x = here["x"]
    factor = math.log2(math.e) / math.sqrt(HDIM)
    flat_out = o_units.reshape(2 * TOK, HDIM)
    heads = []
    for h in range(2):
        keys = wide[1, pl.ds(h, TOK, stride=2), :].astype(jnp.bfloat16)
        values = wide[2, pl.ds(h, TOK, stride=2), :].astype(jnp.bfloat16)
        heads.append((jnp.concatenate([keys, k_seq[...]], axis=1), values))

    def pair_of(i):
        return (x // 2 + 6 - i) % 4

    def attend(i):
        j = pair_of(i)
        for h, (keys, values) in enumerate(heads):
            q = wide[0, pl.ds(j * 512 + h, 256, stride=2), :].astype(jnp.bfloat16)
            q = jnp.concatenate([q, q_seq[pl.ds(pl.multiple_of(j * 256, 256), 256), :]], axis=1)
            s = lax.dot_general(
                q, keys, (((1,), (1,)), ((), ())), preferred_element_type=jnp.float32
            )
            e = jnp.exp2((s - jnp.max(s, axis=1, keepdims=True)) * factor)
            w = (e * (1.0 / jnp.sum(e, axis=1, keepdims=True))).astype(jnp.bfloat16)
            out_rows[pl.ds(h, 256, stride=2), :] = jnp.dot(
                w, values, preferred_element_type=jnp.float32
            )
        flat_out[pl.ds(pl.multiple_of(j * 512, 512), 512), :] = out_rows[...].astype(jnp.bfloat16)

    stops = (
        (o_units, ret1, ret2, back),
        (o_units, ret1, ret2, back),
        (o_units, ret1, ret3, back),
        (o_units, ret1, ret3, back),
    )

    def rows_at(p, stage):
        j = pair_of(p) if "x" not in PARTS[p][:stage] else (x // 2 + 2 + p) % 4
        return pl.ds(j * 2, 2)

    def back_copy(p, stage):
        axis = PARTS[p][stage]
        at = {"x": rows_at(p, stage)}
        at[axis] = here[axis]
        src, dst = stops[p][stage : stage + 2]
        return pltpu.make_async_copy(view(src, **at), view(dst, **at), rown.at[p, stage])

    def back_send(p, stage):
        axis = PARTS[p][stage]
        src, dst = stops[p][stage : stage + 2]
        sems = (rsend.at[p, stage], rrecv.at[p, stage])
        if axis == "x":
            targets = [pair_of(p) * 2, pair_of(p) * 2 + 1] if p != 2 else [x // 2 * 2 + 1 - x % 2]
            for t in targets:
                send_to(here, "x", t, view(src, x=t), view(dst, x=x), *sems)
        else:
            rows = rows_at(p, stage)
            for step in STEPS[axis]:
                t = (here[axis] + step) % SIZE[axis]
                send_to(
                    here, axis, t, view(src, **{"x": rows, axis: t}),
                    view(dst, **{"x": rows, axis: here[axis]}), *sems,
                )
        if axis != "x" or p == 2:
            back_copy(p, stage).start()

    def back_bytes(p, stage):
        axis = PARTS[p][stage]
        if axis == "x":
            return view(back, x=pl.ds(0, 1 if p == 2 else 2))
        return view(back, **{"x": pl.ds(0, 2), axis: pl.ds(0, SIZE[axis] - 1)})

    def back_wait(p, stage):
        wait_for(back_bytes(p, stage), rrecv.at[p, stage])
        if PARTS[p][stage] != "x" or p == 2:
            back_copy(p, stage).wait()

    def block(i, _):
        attend(i)
        for p in range(4):

            @pl.when(i == p)
            def _(p=p):
                back_send(p, 0)

        return 0

    lax.fori_loop(0, 4, block, 0)
    for stage in (1, 2):
        for p in range(4):
            back_wait(p, stage - 1)
            back_send(p, stage)
    for p in range(4):
        back_wait(p, 2)
    for p in range(4):
        for stage in range(3):
            wait_for(back_bytes(p, stage), rsend.at[p, stage])
    for i in range(3):
        for stage in range(3):
            wait_for(whole(ORDERS[i][stage]), send.at[i, stage])


def unpack_kernel(route_ref, i_ref, o_ref):
    pick = pick_rows(route_ref[pl.ds(lax.axis_index("ulysses"), 1), :]).T.astype(jnp.bfloat16)
    for u in range(16):
        both = jnp.dot(
            pick, i_ref[u * 128 : (u + 1) * 128, :], preferred_element_type=jnp.float32
        ).astype(jnp.bfloat16)
        o_ref[:, u * 256 : u * 256 + 128] = both[:64]
        o_ref[:, u * 256 + 128 : u * 256 + 256] = both[64:]


def shards(queries, keys, values, span_route, seq_lengths):
    route = span_route[0]
    block = pltpu.VMEM(BLOCK, jnp.bfloat16)
    three = pltpu.VMEM((3,) + BLOCK, jnp.bfloat16)
    dma = pltpu.SemaphoreType.DMA
    back = pl.pallas_call(
        main_kernel,
        out_shape=jax.ShapeDtypeStruct(BLOCK, jnp.bfloat16),
        in_specs=[SMEM] + [VMEM] * 4,
        out_specs=VMEM,
        scratch_shapes=[three] * 4
        + [
            pltpu.VMEM((3, 2 * TOK, HDIM), jnp.float32),
            pltpu.VMEM((512, HDIM), jnp.float32),
            pltpu.VMEM((TOK, HDIM), jnp.bfloat16),
            pltpu.VMEM((TOK, HDIM), jnp.bfloat16),
            block, block, block, block,
            dma((3, 3)), dma((3, 4)), dma((3, 4)), dma((3,)), dma((3,)), dma((3, 4)), dma((3, 4)),
            dma((4, 3)), dma((4, 3)), dma((4, 3)),
        ],
        compiler_params=pltpu.CompilerParams(has_side_effects=True, collective_id=1),
        name="dispatch_attend_return",
    )(seq_lengths, route, queries, keys, values)
    return pl.pallas_call(
        unpack_kernel,
        out_shape=jax.ShapeDtypeStruct(queries.shape, jnp.bfloat16),
        in_specs=[VMEM] * 2,
        out_specs=VMEM,
        name="unpack",
    )(route, back.reshape(2 * TOK, HDIM))


def solution(mesh):
    placed = (
        P(("bag", "ulysses"), None),
        P(("bag", "ulysses"), None),
        P(("bag", "ulysses"), None),
        P("bag", None, None),
        P("bag", None),
    )
    return jax.shard_map(
        shards, mesh=mesh, in_specs=placed, out_specs=P(("bag", "ulysses"), None), check_vma=False
    )
```

```python
import math

import jax
import jax.numpy as jnp
from jax import lax
from jax.experimental import pallas as pl
from jax.experimental.pallas import tpu as pltpu
from jax.sharding import PartitionSpec as P

HEADS = 32
HDIM = 128
NX, NY, NZ = 8, 8, 16
TOK = NX * NY * NZ
BIG = 1e30
UNIT = (2, HDIM)
BLOCK = (NX, NY, NZ) + UNIT
MESH = pl.DeviceIdType.MESH
VMEM = pl.BlockSpec(memory_space=pltpu.VMEM)
SMEM = pl.BlockSpec(memory_space=pltpu.SMEM)


def pick_rows(route):
    lane_route = jnp.concatenate([route, route], axis=1)
    row = lax.broadcasted_iota(jnp.int32, (128, 128), 0)
    lane = lax.broadcasted_iota(jnp.int32, (128, 128), 1)
    return ((lane_route == row // 2) & (lane // 64 == row % 2)).astype(jnp.float32)


def div(a, n):
    return lax.div(a, jnp.int32(n))


def rem(a, n):
    return lax.rem(a, jnp.int32(n))


def place():
    b = lax.axis_index("bag")
    u = lax.axis_index("ulysses")
    return {"x": div(u, 2), "y": rem(u, 2) * 4 + div(b, 16), "z": rem(b, 16)}


def device(here, axis, t):
    at = dict(here)
    at[axis] = t
    return (rem(at["y"], 4) * 16 + at["z"], at["x"] * 2 + div(at["y"], 4))


def view(ref, **at):
    return ref.at[tuple(at.get(axis, slice(None)) for axis in "xyz")]


SIZE = {"x": NX, "y": NY, "z": NZ}
STEPS = (4, 3, 5, 2, 6, 1, 7)
ORDERS = ("xyz", "yzx", "zxy")
PARTS = ("xyz", "yzx", "zxy", "zxy")
GROUPS = 4
OFFSETS = (2, 1, 3, 0)


def others(here, axis):
    mine = here[axis]
    if axis != "z":
        return [rem(mine + step, 8) for step in STEPS]
    chip, core = div(mine, 2), rem(mine, 2)
    chips = [rem(chip + step, 8) * 2 for step in STEPS]
    return [c + k for c in chips for k in (core, 1 - core)] + [chip * 2 + 1 - core]


def send_to(here, axis, t, src, dst, send, recv):
    pltpu.make_async_remote_copy(
        src_ref=src,
        dst_ref=dst,
        send_sem=send,
        recv_sem=recv,
        device_id=device(here, axis, t),
        device_id_type=MESH,
    ).start()


def wait_for(ref, sem):
    pltpu.make_async_copy(ref, ref, sem).wait()


def main_kernel(
    len_ref, route_ref, q_ref, k_ref, v_ref, back,
    tokens, units, mid1, mid2, fin, wide, rows32, q_seq, keys, values, o_units, ret1, ret2, ret3,
    load, send, recv1, recv2, recv3, own1, own2, own3, rsend, rrecv, rown,
):
    loads = [
        pltpu.make_async_copy(ref, tokens.at[i], load.at[i])
        for i, ref in enumerate((q_ref, k_ref, v_ref))
    ]
    for copy in loads:
        copy.start()
    here = place()
    barrier = pltpu.get_barrier_semaphore()
    peers = {axis: others(here, axis) for axis in "xyz"}
    for axis in "xyz":
        for t in peers[axis]:
            pl.semaphore_signal(
                barrier, inc=1, device_id=device(here, axis, t), device_id_type=MESH
            )

    pick = pick_rows(route_ref[pl.ds(lax.axis_index("ulysses"), 1), :]).astype(jnp.bfloat16)

    def whole(axis):
        return view(fin.at[0], **{axis: pl.ds(0, SIZE[axis] - 1)})

    def group(i, off):
        axis = ORDERS[i][0]
        width = SIZE[axis] // GROUPS
        j = rem(div(here[axis], width) + GROUPS - off, GROUPS)
        return axis, width, j, pl.ds(j * width, width)

    def send1(i):
        axis = ORDERS[i][0]
        mine, width = here[axis], SIZE[axis] // GROUPS
        at_mine = {axis: mine}
        ours = div(mine, width)
        for off in OFFSETS:
            j = rem(ours + off, GROUPS)
            for r in range(0 if off else 1, width):
                t = j * width + (r if off else rem(mine + r, width))
                send_to(
                    here, axis, t, view(units.at[i], **{axis: t}), view(mid1.at[i], **at_mine),
                    send.at[i, 0], recv1.at[i, ours],
                )
        copy1(i).start()

    def copy1(i):
        at_mine = {ORDERS[i][0]: here[ORDERS[i][0]]}
        return pltpu.make_async_copy(
            view(units.at[i], **at_mine), view(mid1.at[i], **at_mine), own1.at[i]
        )

    def send2(i, off):
        first, width, j, rows = group(i, off)
        axis = ORDERS[i][1]
        if off:
            wait_for(view(mid1.at[i], **{first: rows}), recv1.at[i, j])
        else:
            wait_for(view(mid1.at[i], **{first: pl.ds(0, width - 1)}), recv1.at[i, j])
            copy1(i).wait()
        for t in peers[axis]:
            send_to(
                here, axis, t, view(mid1.at[i], **{first: rows, axis: t}),
                view(mid2.at[i], **{first: rows, axis: here[axis]}), send.at[i, 1], recv2.at[i, j],
            )
        copy2(i, off).start()

    def copy2(i, off):
        first, _, j, rows = group(i, off)
        at = {first: rows, ORDERS[i][1]: here[ORDERS[i][1]]}
        return pltpu.make_async_copy(view(mid1.at[i], **at), view(mid2.at[i], **at), own2.at[i, j])

    def send3(i, off):
        first, _, j, rows = group(i, off)
        second, axis = ORDERS[i][1:]
        wait_for(view(mid2.at[i], **{first: rows, second: pl.ds(0, SIZE[second] - 1)}), recv2.at[i, j])
        copy2(i, off).wait()
        for t in peers[axis]:
            send_to(
                here, axis, t, view(mid2.at[i], **{first: rows, axis: t}),
                view(fin.at[i], **{first: rows, axis: here[axis]}), send.at[i, 2], recv3.at[i],
            )
        copy3(i, off).start()

    def copy3(i, off):
        first, _, j, rows = group(i, off)
        at = {first: rows, ORDERS[i][2]: here[ORDERS[i][2]]}
        return pltpu.make_async_copy(view(mid2.at[i], **at), view(fin.at[i], **at), own3.at[i, j])

    for i in range(3):
        loads[i].wait()
        in_ref = tokens.at[i]
        flat = units.at[i].reshape(2 * TOK, HDIM)
        for u in range(0, 16, 2):
            c = u * 256
            halves = [
                jnp.concatenate(
                    [in_ref[:, c + h * 128 : c + h * 128 + 128],
                     in_ref[:, c + 256 + h * 128 : c + 384 + h * 128]], axis=1
                )
                for h in range(2)
            ]
            rows = jnp.dot(
                pick, jnp.concatenate(halves, axis=0), preferred_element_type=jnp.float32
            ).astype(jnp.bfloat16)
            flat[u * 128 : (u + 1) * 128, :] = rows[:, :128]
            flat[(u + 1) * 128 : (u + 2) * 128, :] = rows[:, 128:]
        if i == 0:
            pl.semaphore_wait(barrier, sum(SIZE.values()) - 3)
        send1(i)

    pos = lax.broadcasted_iota(jnp.int32, (TOK, HDIM), 0)
    lane = lax.broadcasted_iota(jnp.int32, (TOK, HDIM), 1)
    first = 0
    inside = jnp.zeros((TOK, HDIM), jnp.bool_)
    for e in range(4):
        last = first + len_ref[0, e]
        inside = inside | ((lane == e) & (pos >= first) & (pos < last))
        first = last
    q_seq[...] = jnp.where(inside, 1.0, 0.0).astype(jnp.bfloat16)
    outside = jnp.where(inside | (lane >= 4), 0.0, -BIG).astype(jnp.bfloat16)
    for h in range(2):
        keys[h, :, HDIM:] = outside

    for send_on in (send2, send3):
        for off in OFFSETS:
            for i in range(3):
                send_on(i, off)
    for i in (1, 2, 0):
        wait_for(whole(ORDERS[i][2]), recv3.at[i])
        for off in OFFSETS:
            copy3(i, off).wait()
        if i:
            wide[i - 1] = fin.at[i].reshape(2 * TOK, HDIM)[...].astype(jnp.float32)
            for h in range(2):
                head = wide[i - 1, pl.ds(h, TOK, stride=2), :].astype(jnp.bfloat16)
                if i == 1:
                    keys[h, :, :HDIM] = head
                else:
                    values[h] = head

    x = here["x"]
    factor = math.log2(math.e) / math.sqrt(HDIM)
    flat_out = o_units.reshape(2 * TOK, HDIM)
    flat_in = fin.at[0].reshape(2 * TOK, HDIM)

    def pair_of(i):
        return rem(div(x, 2) + 6 - i, 4)

    def attend(i):
        j = pair_of(i)
        here_rows = pl.ds(pl.multiple_of(j * 512, 512), 512)
        rows32[0] = flat_in[here_rows, :].astype(jnp.float32)
        seq = q_seq[pl.ds(pl.multiple_of(j * 256, 256), 256), :]
        for h in range(2):
            q = rows32[0, pl.ds(h, 256, stride=2), :].astype(jnp.bfloat16)
            s = lax.dot_general(
                jnp.concatenate([q, seq], axis=1), keys[h], (((1,), (1,)), ((), ())),
                preferred_element_type=jnp.float32,
            )
            e = jnp.exp2((s - jnp.max(s, axis=1, keepdims=True)) * factor)
            w = (e * (1.0 / jnp.sum(e, axis=1, keepdims=True))).astype(jnp.bfloat16)
            rows32[1, pl.ds(h, 256, stride=2), :] = jnp.dot(
                w, values[h], preferred_element_type=jnp.float32
            )
        flat_out[here_rows, :] = rows32[1].astype(jnp.bfloat16)

    stops = (
        (o_units, ret1, ret2, back),
        (o_units, ret1, ret2, back),
        (o_units, ret1, ret3, back),
        (o_units, ret1, ret3, back),
    )

    def rows_at(p, stage):
        j = pair_of(p) if "x" not in PARTS[p][:stage] else rem(div(x, 2) + 2 + p, 4)
        return pl.ds(j * 2, 2)

    def back_copy(p, stage):
        axis = PARTS[p][stage]
        at = {"x": rows_at(p, stage)}
        at[axis] = here[axis]
        src, dst = stops[p][stage : stage + 2]
        return pltpu.make_async_copy(view(src, **at), view(dst, **at), rown.at[p, stage])

    def back_send(p, stage):
        axis = PARTS[p][stage]
        src, dst = stops[p][stage : stage + 2]
        sems = (rsend.at[p, stage], rrecv.at[p, stage])
        if axis == "x":
            targets = [pair_of(p) * 2, pair_of(p) * 2 + 1] if p != 2 else [x + 1 - rem(x, 2) * 2]
            for t in targets:
                send_to(here, "x", t, view(src, x=t), view(dst, x=x), *sems)
        else:
            rows = rows_at(p, stage)
            for t in peers[axis]:
                send_to(
                    here, axis, t, view(src, **{"x": rows, axis: t}),
                    view(dst, **{"x": rows, axis: here[axis]}), *sems,
                )
        if axis != "x" or p == 2:
            back_copy(p, stage).start()

    def back_bytes(p, stage):
        axis = PARTS[p][stage]
        if axis == "x":
            return view(back, x=pl.ds(0, 1 if p == 2 else 2))
        return view(back, **{"x": pl.ds(0, 2), axis: pl.ds(0, SIZE[axis] - 1)})

    def back_wait(p, stage):
        wait_for(back_bytes(p, stage), rrecv.at[p, stage])
        if PARTS[p][stage] != "x" or p == 2:
            back_copy(p, stage).wait()

    def block(i, _):
        attend(i)
        for p in range(4):

            @pl.when(i == p)
            def _(p=p):
                back_send(p, 0)

        return 0

    lax.fori_loop(0, 4, block, 0)
    for stage in (1, 2):
        for p in range(4):
            back_wait(p, stage - 1)
            back_send(p, stage)
    for p in range(4):
        back_wait(p, 2)
    for p in range(4):
        for stage in range(3):
            wait_for(back_bytes(p, stage), rsend.at[p, stage])
    for i in range(3):
        for stage in range(3):
            wait_for(whole(ORDERS[i][stage]), send.at[i, stage])


def unpack_kernel(route_ref, i_ref, o_ref):
    pick = pick_rows(route_ref[pl.ds(lax.axis_index("ulysses"), 1), :]).T.astype(jnp.bfloat16)
    for u in range(4):
        both = jnp.dot(
            pick, i_ref[u * 128 : (u + 1) * 128, :], preferred_element_type=jnp.float32
        ).astype(jnp.bfloat16)
        o_ref[:, u * 256 : u * 256 + 128] = both[:64]
        o_ref[:, u * 256 + 128 : u * 256 + 256] = both[64:]


def shards(queries, keys, values, span_route, seq_lengths):
    route = span_route[0]
    block = pltpu.VMEM(BLOCK, jnp.bfloat16)
    three = pltpu.VMEM((3,) + BLOCK, jnp.bfloat16)
    dma = pltpu.SemaphoreType.DMA
    back = pl.pallas_call(
        main_kernel,
        out_shape=jax.ShapeDtypeStruct(BLOCK, jnp.bfloat16),
        in_specs=[SMEM, VMEM] + [pl.BlockSpec(memory_space=pl.ANY)] * 3,
        out_specs=VMEM,
        scratch_shapes=[pltpu.VMEM((3,) + queries.shape, jnp.bfloat16)]
        + [three] * 4
        + [
            pltpu.VMEM((2, 2 * TOK, HDIM), jnp.float32),
            pltpu.VMEM((2, 512, HDIM), jnp.float32),
            pltpu.VMEM((TOK, HDIM), jnp.bfloat16),
            pltpu.VMEM((2, TOK, 2 * HDIM), jnp.bfloat16),
            pltpu.VMEM((2, TOK, HDIM), jnp.bfloat16),
            block, block, block, block,
            dma((3,)), dma((3, 3)), dma((3, 4)), dma((3, 4)), dma((3,)), dma((3,)), dma((3, 4)), dma((3, 4)),
            dma((4, 3)), dma((4, 3)), dma((4, 3)),
        ],
        compiler_params=pltpu.CompilerParams(has_side_effects=True, collective_id=1),
        name="dispatch_attend_return",
    )(seq_lengths, route, queries, keys, values)
    return pl.pallas_call(
        unpack_kernel,
        out_shape=jax.ShapeDtypeStruct(queries.shape, jnp.bfloat16),
        grid=(4,),
        in_specs=[
            pl.BlockSpec((16, 64), lambda i: (0, 0)),
            pl.BlockSpec((512, HDIM), lambda i: (i, 0)),
        ],
        out_specs=pl.BlockSpec((64, 1024), lambda i: (0, i)),
        name="unpack",
    )(route, back.reshape(2 * TOK, HDIM))


def solution(mesh):
    placed = (
        P(("bag", "ulysses"), None),
        P(("bag", "ulysses"), None),
        P(("bag", "ulysses"), None),
        P("bag", None, None),
        P("bag", None),
    )
    return jax.shard_map(
        shards, mesh=mesh, in_specs=placed, out_specs=P(("bag", "ulysses"), None), check_vma=False
    )
```

```python
import math

import jax
import jax.numpy as jnp
from jax import lax
from jax.experimental import pallas as pl
from jax.experimental.pallas import tpu as pltpu
from jax.sharding import PartitionSpec as P

HEADS = 32
HDIM = 128
NX, NY, NZ = 8, 8, 16
TOK = NX * NY * NZ
BIG = 1e30
UNIT = (2, HDIM)
BLOCK = (NX, NY, NZ) + UNIT
MESH = pl.DeviceIdType.MESH
VMEM = pl.BlockSpec(memory_space=pltpu.VMEM)
SMEM = pl.BlockSpec(memory_space=pltpu.SMEM)


def pick_rows(route):
    lane_route = jnp.concatenate([route, route], axis=1)
    row = lax.broadcasted_iota(jnp.int32, (128, 128), 0)
    lane = lax.broadcasted_iota(jnp.int32, (128, 128), 1)
    return ((lane_route == row // 2) & (lane // 64 == row % 2)).astype(jnp.float32)


def div(a, n):
    return lax.div(a, jnp.int32(n))


def rem(a, n):
    return lax.rem(a, jnp.int32(n))


def place():
    b = lax.axis_index("bag")
    u = lax.axis_index("ulysses")
    return {"x": div(u, 2), "y": rem(u, 2) * 4 + div(b, 16), "z": rem(b, 16)}


def device(here, axis, t):
    at = dict(here)
    at[axis] = t
    return (rem(at["y"], 4) * 16 + at["z"], at["x"] * 2 + div(at["y"], 4))


def view(ref, **at):
    return ref.at[tuple(at.get(axis, slice(None)) for axis in "xyz")]


SIZE = {"x": NX, "y": NY, "z": NZ}
STEPS = (4, 3, 5, 2, 6, 1, 7)
ORDERS = ("xyz", "yzx", "zxy")
PARTS = ("xyz", "yzx", "zxy", "yxz")
GROUPS = 4
OFFSETS = (2, 1, 3, 0)


def others(here, axis):
    mine = here[axis]
    if axis != "z":
        return [rem(mine + step, 8) for step in STEPS]
    chip, core = div(mine, 2), rem(mine, 2)
    chips = [rem(chip + step, 8) * 2 for step in STEPS]
    return [c + k for c in chips for k in (core, 1 - core)] + [chip * 2 + 1 - core]


def send_to(here, axis, t, src, dst, send, recv):
    pltpu.make_async_remote_copy(
        src_ref=src,
        dst_ref=dst,
        send_sem=send,
        recv_sem=recv,
        device_id=device(here, axis, t),
        device_id_type=MESH,
    ).start()


def wait_for(ref, sem):
    pltpu.make_async_copy(ref, ref, sem).wait()


def main_kernel(
    len_ref, route_ref, q_ref, k_ref, v_ref, back,
    tokens, units, mid1, mid2, fin, wide, rows32, q_seq, keys, values, o_units, ret1, ret2, ret3,
    load, send, recv1, recv2, recv3, own1, own2, own3, rsend, rrecv, rown,
):
    loads = [
        pltpu.make_async_copy(ref, tokens.at[i], load.at[i])
        for i, ref in enumerate((q_ref, k_ref, v_ref))
    ]
    for copy in loads:
        copy.start()
    here = place()
    barrier = pltpu.get_barrier_semaphore()
    peers = {axis: others(here, axis) for axis in "xyz"}
    for axis in "xyz":
        for t in peers[axis]:
            pl.semaphore_signal(
                barrier, inc=1, device_id=device(here, axis, t), device_id_type=MESH
            )

    pick = pick_rows(route_ref[pl.ds(lax.axis_index("ulysses"), 1), :]).astype(jnp.bfloat16)

    def whole(axis):
        return view(fin.at[0], **{axis: pl.ds(0, SIZE[axis] - 1)})

    def group(i, off):
        axis = ORDERS[i][0]
        width = SIZE[axis] // GROUPS
        j = rem(div(here[axis], width) + GROUPS - off, GROUPS)
        return axis, width, j, pl.ds(j * width, width)

    def send1(i):
        axis = ORDERS[i][0]
        mine, width = here[axis], SIZE[axis] // GROUPS
        at_mine = {axis: mine}
        ours = div(mine, width)
        for off in OFFSETS:
            j = rem(ours + off, GROUPS)
            for r in range(0 if off else 1, width):
                t = j * width + (r if off else rem(mine + r, width))
                send_to(
                    here, axis, t, view(units.at[i], **{axis: t}), view(mid1.at[i], **at_mine),
                    send.at[i, 0], recv1.at[i, ours],
                )
        copy1(i).start()

    def copy1(i):
        at_mine = {ORDERS[i][0]: here[ORDERS[i][0]]}
        return pltpu.make_async_copy(
            view(units.at[i], **at_mine), view(mid1.at[i], **at_mine), own1.at[i]
        )

    def send2(i, off):
        first, width, j, rows = group(i, off)
        axis = ORDERS[i][1]
        if off:
            wait_for(view(mid1.at[i], **{first: rows}), recv1.at[i, j])
        else:
            wait_for(view(mid1.at[i], **{first: pl.ds(0, width - 1)}), recv1.at[i, j])
            copy1(i).wait()
        for t in peers[axis]:
            send_to(
                here, axis, t, view(mid1.at[i], **{first: rows, axis: t}),
                view(mid2.at[i], **{first: rows, axis: here[axis]}), send.at[i, 1], recv2.at[i, j],
            )
        copy2(i, off).start()

    def copy2(i, off):
        first, _, j, rows = group(i, off)
        at = {first: rows, ORDERS[i][1]: here[ORDERS[i][1]]}
        return pltpu.make_async_copy(view(mid1.at[i], **at), view(mid2.at[i], **at), own2.at[i, j])

    def send3(i, off):
        first, _, j, rows = group(i, off)
        second, axis = ORDERS[i][1:]
        wait_for(view(mid2.at[i], **{first: rows, second: pl.ds(0, SIZE[second] - 1)}), recv2.at[i, j])
        copy2(i, off).wait()
        for t in peers[axis]:
            send_to(
                here, axis, t, view(mid2.at[i], **{first: rows, axis: t}),
                view(fin.at[i], **{first: rows, axis: here[axis]}), send.at[i, 2], recv3.at[i],
            )
        copy3(i, off).start()

    def copy3(i, off):
        first, _, j, rows = group(i, off)
        at = {first: rows, ORDERS[i][2]: here[ORDERS[i][2]]}
        return pltpu.make_async_copy(view(mid2.at[i], **at), view(fin.at[i], **at), own3.at[i, j])

    for i in range(3):
        loads[i].wait()
        in_ref = tokens.at[i]
        flat = units.at[i].reshape(2 * TOK, HDIM)
        for u in range(0, 16, 2):
            c = u * 256
            halves = [
                jnp.concatenate(
                    [in_ref[:, c + h * 128 : c + h * 128 + 128],
                     in_ref[:, c + 256 + h * 128 : c + 384 + h * 128]], axis=1
                )
                for h in range(2)
            ]
            rows = jnp.dot(
                pick, jnp.concatenate(halves, axis=0), preferred_element_type=jnp.float32
            ).astype(jnp.bfloat16)
            flat[u * 128 : (u + 1) * 128, :] = rows[:, :128]
            flat[(u + 1) * 128 : (u + 2) * 128, :] = rows[:, 128:]
        if i == 0:
            pl.semaphore_wait(barrier, sum(SIZE.values()) - 3)
        send1(i)

    pos = lax.broadcasted_iota(jnp.int32, (TOK, HDIM), 0)
    lane = lax.broadcasted_iota(jnp.int32, (TOK, HDIM), 1)
    first = 0
    inside = jnp.zeros((TOK, HDIM), jnp.bool_)
    for e in range(4):
        last = first + len_ref[0, e]
        inside = inside | ((lane == e) & (pos >= first) & (pos < last))
        first = last
    q_seq[...] = jnp.where(inside, 1.0, 0.0).astype(jnp.bfloat16)
    outside = jnp.where(inside | (lane >= 4), 0.0, -BIG).astype(jnp.bfloat16)
    for h in range(2):
        keys[h, :, HDIM:] = outside

    for send_on in (send2, send3):
        for off in OFFSETS:
            for i in range(3):
                send_on(i, off)
    for i in (1, 2, 0):
        wait_for(whole(ORDERS[i][2]), recv3.at[i])
        for off in OFFSETS:
            copy3(i, off).wait()
        if i:
            wide[i - 1] = fin.at[i].reshape(2 * TOK, HDIM)[...].astype(jnp.float32)
            for h in range(2):
                head = wide[i - 1, pl.ds(h, TOK, stride=2), :].astype(jnp.bfloat16)
                if i == 1:
                    keys[h, :, :HDIM] = head
                else:
                    values[h] = head

    x = here["x"]
    factor = math.log2(math.e) / math.sqrt(HDIM)
    flat_out = o_units.reshape(2 * TOK, HDIM)
    flat_in = fin.at[0].reshape(2 * TOK, HDIM)

    def pair_of(i):
        late = div(i, 2)
        return rem(div(x, 2) + (2 - i) * (1 - late) + (9 - i * 3) * late, 4)

    def attend(i):
        j = pair_of(i)
        here_rows = pl.ds(pl.multiple_of(j * 512, 512), 512)
        rows32[0] = flat_in[here_rows, :].astype(jnp.float32)
        seq = q_seq[pl.ds(pl.multiple_of(j * 256, 256), 256), :]
        for h in range(2):
            q = rows32[0, pl.ds(h, 256, stride=2), :].astype(jnp.bfloat16)
            s = lax.dot_general(
                jnp.concatenate([q, seq], axis=1), keys[h], (((1,), (1,)), ((), ())),
                preferred_element_type=jnp.float32,
            )
            e = jnp.exp2((s - jnp.max(s, axis=1, keepdims=True)) * factor)
            w = (e * (1.0 / jnp.sum(e, axis=1, keepdims=True))).astype(jnp.bfloat16)
            rows32[1, pl.ds(h, 256, stride=2), :] = jnp.dot(
                w, values[h], preferred_element_type=jnp.float32
            )
        flat_out[here_rows, :] = rows32[1].astype(jnp.bfloat16)

    stops = (
        (o_units, ret1, ret2, back),
        (o_units, ret1, ret2, back),
        (o_units, ret1, ret3, back),
        (o_units, ret1, ret2, back),
    )

    def rows_at(p, stage):
        j = pair_of(p) if "x" not in PARTS[p][:stage] else rem(div(x, 2) + (2, 3, 1, 0)[p], 4)
        return pl.ds(j * 2, 2)

    def back_copy(p, stage):
        axis = PARTS[p][stage]
        at = {"x": rows_at(p, stage)}
        at[axis] = here[axis]
        src, dst = stops[p][stage : stage + 2]
        return pltpu.make_async_copy(view(src, **at), view(dst, **at), rown.at[p, stage])

    def back_send(p, stage):
        axis = PARTS[p][stage]
        src, dst = stops[p][stage : stage + 2]
        sems = (rsend.at[p, stage], rrecv.at[p, stage])
        if axis == "x":
            targets = [pair_of(p) * 2, pair_of(p) * 2 + 1] if p != 3 else [x + 1 - rem(x, 2) * 2]
            for t in targets:
                send_to(here, "x", t, view(src, x=t), view(dst, x=x), *sems)
        else:
            rows = rows_at(p, stage)
            for t in peers[axis]:
                send_to(
                    here, axis, t, view(src, **{"x": rows, axis: t}),
                    view(dst, **{"x": rows, axis: here[axis]}), *sems,
                )
        if axis != "x" or p == 3:
            back_copy(p, stage).start()

    def back_bytes(p, stage):
        axis = PARTS[p][stage]
        if axis == "x":
            return view(back, x=pl.ds(0, 1 if p == 3 else 2))
        return view(back, **{"x": pl.ds(0, 2), axis: pl.ds(0, SIZE[axis] - 1)})

    def back_wait(p, stage):
        wait_for(back_bytes(p, stage), rrecv.at[p, stage])
        if PARTS[p][stage] != "x" or p == 3:
            back_copy(p, stage).wait()

    def block(i, _):
        attend(i)
        for p in range(4):

            @pl.when(i == p)
            def _(p=p):
                back_send(p, 0)

        return 0

    lax.fori_loop(0, 4, block, 0)
    for stage, parts in ((1, (0, 1, 2, 3)), (2, (3, 1, 0, 2))):
        for p in parts:
            back_wait(p, stage - 1)
            back_send(p, stage)
    for p in range(4):
        back_wait(p, 2)
    for p in range(4):
        for stage in range(3):
            wait_for(back_bytes(p, stage), rsend.at[p, stage])
    for i in range(3):
        for stage in range(3):
            wait_for(whole(ORDERS[i][stage]), send.at[i, stage])


def unpack_kernel(route_ref, i_ref, o_ref):
    pick = pick_rows(route_ref[pl.ds(lax.axis_index("ulysses"), 1), :]).T.astype(jnp.bfloat16)
    for u in range(16):
        both = jnp.dot(
            pick, i_ref[u * 128 : (u + 1) * 128, :], preferred_element_type=jnp.float32
        ).astype(jnp.bfloat16)
        o_ref[:, u * 256 : u * 256 + 128] = both[:64]
        o_ref[:, u * 256 + 128 : u * 256 + 256] = both[64:]


def shards(queries, keys, values, span_route, seq_lengths):
    route = span_route[0]
    block = pltpu.VMEM(BLOCK, jnp.bfloat16)
    three = pltpu.VMEM((3,) + BLOCK, jnp.bfloat16)
    dma = pltpu.SemaphoreType.DMA
    back = pl.pallas_call(
        main_kernel,
        out_shape=jax.ShapeDtypeStruct(BLOCK, jnp.bfloat16),
        in_specs=[SMEM, VMEM] + [pl.BlockSpec(memory_space=pl.ANY)] * 3,
        out_specs=VMEM,
        scratch_shapes=[pltpu.VMEM((3,) + queries.shape, jnp.bfloat16)]
        + [three] * 4
        + [
            pltpu.VMEM((2, 2 * TOK, HDIM), jnp.float32),
            pltpu.VMEM((2, 512, HDIM), jnp.float32),
            pltpu.VMEM((TOK, HDIM), jnp.bfloat16),
            pltpu.VMEM((2, TOK, 2 * HDIM), jnp.bfloat16),
            pltpu.VMEM((2, TOK, HDIM), jnp.bfloat16),
            block, block, block, block,
            dma((3,)), dma((3, 3)), dma((3, 4)), dma((3, 4)), dma((3,)), dma((3,)), dma((3, 4)), dma((3, 4)),
            dma((4, 3)), dma((4, 3)), dma((4, 3)),
        ],
        compiler_params=pltpu.CompilerParams(has_side_effects=True, collective_id=1),
        name="dispatch_attend_return",
    )(seq_lengths, route, queries, keys, values)
    return pl.pallas_call(
        unpack_kernel,
        out_shape=jax.ShapeDtypeStruct(queries.shape, jnp.bfloat16),
        in_specs=[VMEM] * 2,
        out_specs=VMEM,
        name="unpack",
    )(route, back.reshape(2 * TOK, HDIM))


def solution(mesh):
    placed = (
        P(("bag", "ulysses"), None),
        P(("bag", "ulysses"), None),
        P(("bag", "ulysses"), None),
        P("bag", None, None),
        P("bag", None),
    )
    return jax.shard_map(
        shards, mesh=mesh, in_specs=placed, out_specs=P(("bag", "ulysses"), None), check_vma=False
    )
```
